32 devices in a mesh: grp: 2 (over y), blk: 8 (over z, x), seq: 1, ch: 2 (over core).
Axes of the slice: x: 2, y: 2, z: 4, core: 2. Of those that a mesh axis runs over, the one named last changes fastest.
Arguments:
- alignment_activity: bfloat16 [512, 128, 64], P(('grp', 'seq'), 'blk'), parts along dimension 0, may hold values from -40 to 40
- sequence_mask: int32 [512], P('grp'), parts along dimension 0, may hold values 0 or 1
- residue_mask: int32 [256], P('grp'), parts along dimension 0, may hold values 0 or 1
- lower_weights: bfloat16 [64, 32], replicated, may hold values from -0.75 to 0.75
- upper_weights: bfloat16 [64, 32], replicated, may hold values from -0.75 to 0.75
- output_projector: bfloat16 [1024, 128], replicated, may hold values from -0.1875 to 0.1875
Outputs:
- pair_update: bfloat16 [128, 256, 128], P('ch', ('grp', 'blk'), 'seq'), parts along dimension 1
The draws below stay inside these ranges and needn't reach their ends.
There are 2 independent parts, one for each index of `grp`. The reference program is written for one: setup_inputs(seed, part) draws one part's arguments, and reference() takes and returns one part's arrays. A program takes and returns all parts, laid end to end along the dimension named above; an argument that names none is the same for every part. Nothing has to cross between parts.
All inputs are finite; a program needn't handle non-finite values.
Results may differ from the reference program's by a relative error of at most 0.012.
Values may be sent and summed in bfloat16 or wider, within the bound.
A program may use at most 64 MiB of HBM per device.

```python
import jax
import jax.numpy as jnp
from jax import lax

FEATURE_DEPTH = 64
REDUCED_DEPTH = 32
PAIR = 128
BLOCK_RESIDUES = 16
CHAIN_LENGTH = 128
HOMOLOG_NUMBER = 256
N_SEQ = 1


def draw_alignment_activity(key, part):
    initial_random_seed, another_random_seed = jax.random.split(jax.random.fold_in(key, 17), 2)
    timing_report = jnp.clip(jax.random.normal(initial_random_seed, (CHAIN_LENGTH, FEATURE_DEPTH), jnp.float32), -6.0, 6.0) * 0.6
    random_shift = jnp.clip(jax.random.normal(another_random_seed, (HOMOLOG_NUMBER, CHAIN_LENGTH, FEATURE_DEPTH), jnp.float32), -8.0, 8.0)
    return (timing_report[None] + random_shift).astype(jnp.bfloat16)


def set_ends(entries, rng, smallest, largest):
    index_at = [jax.random.randint(jax.random.fold_in(rng, axis), (), 0, length) for axis, length in enumerate(entries.shape)]
    main_axis = entries.shape.index(max(entries.shape))
    next_to = index_at[:main_axis] + [(index_at[main_axis] + 1) % entries.shape[main_axis]] + index_at[main_axis + 1:]
    return entries.at[tuple(index_at)].set(smallest).at[tuple(next_to)].set(largest)


def noise(key, extent, scale, most, held_as=jnp.bfloat16):
    result = jax.random.normal(key, extent, jnp.float32) * scale
    return jnp.minimum(jnp.maximum(result, -most), most).astype(held_as)


def setup_inputs(seed: int = 0, part: int = 0) -> dict:
    streams_of = jax.random.split(jax.random.key(seed), 7)
    part_splits = jax.random.split(jax.random.fold_in(streams_of[6], part), 7)
    alignment_activity = draw_alignment_activity(jax.random.fold_in(jax.random.fold_in(streams_of[6], part), 71), part)
    sequence_mask = set_ends((jax.random.randint(part_splits[1], (HOMOLOG_NUMBER,), 0, 4) < 3).astype(jnp.int32), jax.random.fold_in(part_splits[1], 1), 0, 1)
    residue_mask = set_ends((jax.random.randint(part_splits[2], (CHAIN_LENGTH,), 0, 4) < 3).astype(jnp.int32), jax.random.fold_in(part_splits[2], 1), 0, 1)
    lower_weights = noise(streams_of[3], (FEATURE_DEPTH, REDUCED_DEPTH), FEATURE_DEPTH ** -0.5, 0.75)
    upper_weights = noise(streams_of[4], (FEATURE_DEPTH, REDUCED_DEPTH), FEATURE_DEPTH ** -0.5, 0.75)
    output_projector = noise(streams_of[5], (REDUCED_DEPTH * REDUCED_DEPTH, PAIR), (REDUCED_DEPTH * REDUCED_DEPTH) ** -0.5, 0.1875)
    return {"alignment_activity": alignment_activity, "sequence_mask": sequence_mask, "residue_mask": residue_mask, "lower_weights": lower_weights, "upper_weights": upper_weights, "output_projector": output_projector}


def reference(alignment_activity, sequence_mask, residue_mask, lower_weights, upper_weights, output_projector):
    value_entries = alignment_activity.astype(jnp.float32)
    centred = value_entries - lax.optimization_barrier(jnp.mean(value_entries, axis=-1, keepdims=True))
    variance = lax.optimization_barrier(jnp.mean(centred * centred, axis=-1, keepdims=True))
    normed = (centred * lax.rsqrt(variance + 1e-05)).astype(jnp.bfloat16)
    weight = sequence_mask.astype(jnp.float32)[:, None, None] * residue_mask.astype(jnp.float32)[None, :, None]
    normed_wide = normed.astype(jnp.float32)
    left_matrix = (jnp.einsum('sic,cd->sid', normed_wide, lower_weights.astype(jnp.float32)) * weight).astype(jnp.bfloat16)
    right = (jnp.einsum('sic,cd->sid', normed_wide, upper_weights.astype(jnp.float32)) * weight).astype(jnp.bfloat16)
    portion_rows = HOMOLOG_NUMBER // N_SEQ
    table = output_projector.astype(jnp.float32).reshape(REDUCED_DEPTH, REDUCED_DEPTH, PAIR)
    right_wide = right.astype(jnp.float32)
    left_block_list = left_matrix.reshape(HOMOLOG_NUMBER, CHAIN_LENGTH // BLOCK_RESIDUES, BLOCK_RESIDUES, REDUCED_DEPTH).transpose(1, 0, 2, 3)

    def one_block(left_rows):
        total = jnp.zeros((PAIR, BLOCK_RESIDUES, CHAIN_LENGTH), jnp.float32)
        for quarter in range(N_SEQ):
            left_part = left_rows[quarter * portion_rows:(quarter + 1) * portion_rows].astype(jnp.float32)
            right_part = right_wide[quarter * portion_rows:(quarter + 1) * portion_rows]
            outer = jnp.einsum('sic,sjd->ijcd', left_part, right_part).astype(jnp.bfloat16)
            outer = lax.optimization_barrier(outer).astype(jnp.float32)
            total = total + jnp.einsum('ijcd,cde->eij', outer, table)
        return total
    stacked = lax.map(one_block, left_block_list)
    pair_sum = stacked.transpose(1, 0, 2, 3).reshape(PAIR, CHAIN_LENGTH, CHAIN_LENGTH)
    count = jnp.sum(sequence_mask.astype(jnp.float32))
    res_wide = residue_mask.astype(jnp.float32)
    norm = res_wide[:, None] * res_wide[None, :] * count
    return (pair_sum / jnp.maximum(norm, 1.0)[None]).astype(jnp.bfloat16)
```

```python
import functools
import math

import jax
import jax.numpy as jnp
from jax import lax
from jax.experimental import pallas as pl
from jax.experimental.pallas import tpu as pltpu
from jax.sharding import PartitionSpec as P


def shards(
    alignment_activity, sequence_mask, residue_mask, lower_weights, upper_weights, output_projector
):
    local_rows, block_rows, channel_count = alignment_activity.shape
    proj_width = lower_weights.shape[1]
    pair_width = output_projector.shape[1]
    seq_count = lax.axis_size("seq")
    core_count = lax.axis_size("ch")
    seq_place = lax.axis_index("seq")
    blk_place = lax.axis_index("blk")
    core_place = lax.axis_index("ch")
    value_entries = alignment_activity.astype(jnp.float32)
    centred = value_entries - jnp.mean(value_entries, axis=-1, keepdims=True)
    variance = jnp.mean(centred * centred, axis=-1, keepdims=True)
    normed = (centred * lax.rsqrt(variance + 1e-05)).astype(jnp.bfloat16)
    rows_valid = lax.dynamic_slice_in_dim(sequence_mask, seq_place * local_rows, local_rows).astype(
        jnp.float32
    )
    res_valid = lax.dynamic_slice_in_dim(residue_mask, blk_place * block_rows, block_rows).astype(
        jnp.float32
    )
    weight = (rows_valid[:, None] * res_valid[None, :])[:, :, None]
    left_matrix = (
        jnp.einsum("sic,cd->sid", normed, lower_weights, preferred_element_type=jnp.float32)
        * weight
    ).astype(jnp.bfloat16)
    right = (
        jnp.einsum("sic,cd->sid", normed, upper_weights, preferred_element_type=jnp.float32)
        * weight
    ).astype(jnp.bfloat16)
    right_flat = right.reshape(local_rows, block_rows * proj_width)
    table = output_projector.reshape(proj_width, proj_width, pair_width)
    out_width = pair_width // core_count
    table_used = lax.dynamic_slice_in_dim(table, core_place * out_width, out_width, 2)
    used_channels = table_used.shape[2]
    piece = lax.all_gather(right_flat, "blk", axis=1, tiled=True)
    col_count = piece.shape[1] // proj_width
    block_cols = math.gcd(col_count, 128)
    block_count = col_count // block_cols
    stacked = piece.reshape(local_rows, block_count, block_cols, proj_width).transpose(1, 0, 2, 3)

    def one_block(right_part):
        outer = jnp.einsum(
            "sic,sjd->ijcd", left_matrix, right_part, preferred_element_type=jnp.float32
        ).astype(jnp.bfloat16)
        return jnp.einsum("ijcd,cde->eij", outer, table_used, preferred_element_type=jnp.float32)

    results = lax.map(one_block, stacked)
    partial_sum = results.transpose(1, 2, 0, 3).reshape(used_channels, block_rows, col_count)
    all_cols = partial_sum.shape[2]
    quarter_cols = all_cols // seq_count
    summed = lax.psum_scatter(
        partial_sum.astype(jnp.bfloat16), "seq", scatter_dimension=2, tiled=True
    ).astype(jnp.float32)
    count = jnp.sum(sequence_mask.astype(jnp.float32))
    col_valid = lax.dynamic_slice_in_dim(
        residue_mask, seq_place * quarter_cols, quarter_cols
    ).astype(jnp.float32)
    norm = res_valid[:, None] * col_valid[None, :] * count
    return (summed / jnp.maximum(norm, 1.0)[None]).astype(jnp.bfloat16)


F32 = jnp.float32
BF16 = jnp.bfloat16
CHUNKS = 2
MESH = pl.DeviceIdType.MESH


def fused(
    sizes,
    x_ref, srow_ref, jrow_ref, rmask_ref, lower_ref, upper_ref, table_ref,
    out_ref,
    wide, left_t, right_w, right_t, table_w, acc, away, near, inv,
    recv_sem, send_sem, swap_sem,
):
    nblk, rows, res, feat, width = sizes
    half = width // 2
    part = half // CHUNKS
    nz = nblk // 2
    cols = nblk * res
    lane_tiles = rows // 128
    blk = lax.axis_index("blk")
    core = lax.axis_index("ch")
    z = blk // 2
    side = blk % 2
    across = z * 2 + 1 - side

    barrier = pltpu.get_barrier_semaphore()
    pl.semaphore_signal(barrier, inc=1, device_id={"blk": across}, device_id_type=MESH)
    pl.semaphore_signal(barrier, inc=1, device_id={"ch": 1 - core}, device_id_type=MESH)

    @pl.when(z > 0)
    def _():
        pl.semaphore_signal(barrier, inc=1, device_id={"blk": blk - 2}, device_id_type=MESH)

    @pl.when(z < nz - 1)
    def _():
        pl.semaphore_signal(barrier, inc=1, device_id={"blk": blk + 2}, device_id_type=MESH)

    wide[:, :feat] = x_ref[...].astype(F32).reshape(rows * res, feat)
    r_at = lax.broadcasted_iota(jnp.int32, (feat, feat), 0)
    c_at = lax.broadcasted_iota(jnp.int32, (feat, feat), 1)
    centre = (jnp.where(r_at == c_at, 1.0, 0.0) - 1.0 / feat).astype(BF16)
    lower_t = lower_ref[...].astype(F32).T.astype(BF16)
    upper_t = upper_ref[...].astype(F32).T.astype(BF16)
    weights = jnp.concatenate([lower_t, upper_t], axis=0)
    srow = srow_ref[...].astype(F32)
    nt = (((1,), (1,)), ((), ()))
    for i in range(res):
        x_i = wide[pl.ds(i, rows, stride=res), :][:, :feat].astype(BF16)
        cent = lax.dot_general(centre, x_i, nt, preferred_element_type=F32)
        var = jnp.mean(cent * cent, axis=0, keepdims=True)
        normed = (cent * lax.rsqrt(var + 1e-05)).astype(BF16)
        proj = jnp.dot(weights, normed, preferred_element_type=F32)
        proj = proj * (srow * rmask_ref[blk * res + i].astype(F32))
        left_t[i * width:(i + 1) * width, :] = proj[:width].astype(BF16)
        for g in range(lane_tiles):
            right_w[g, pl.ds(i, width, stride=res), :] = proj[width:, g * 128:(g + 1) * 128]
    mine = pl.ds(pl.multiple_of(core * (half * res), half * res), half * res)
    for g in range(lane_tiles):
        block = right_w[g, mine, :].astype(BF16).reshape(half, res, 128)
        right_t[blk, :, :, g * 128:(g + 1) * 128] = block

    peers = 2 + (z + nz - 1) // nz + (2 * nz - 2 - z) // nz
    pl.semaphore_wait(barrier, peers)

    def copy(block, q, way, target):
        ref = right_t.at[block, pl.ds(q * part, part)]
        return pltpu.make_async_remote_copy(
            src_ref=ref, dst_ref=ref,
            send_sem=send_sem.at[way, block, q], recv_sem=recv_sem.at[block, q],
            device_id={"blk": target}, device_id_type=MESH,
        )

    def up(block, q):
        return copy(block, q, 0, blk + 2)

    def down(block, q):
        return copy(block, q, 1, blk - 2)

    def cross(block, q):
        return copy(block, q, 2, across)

    def each_hop(q, hop, act_below, act_above):
        @pl.when(z >= hop)
        def _():
            act_below(blk - 2 * hop, q)

        @pl.when(z + hop < nz)
        def _():
            act_above(blk + 2 * hop, q)

    for q in range(CHUNKS):
        cross(blk, q).start()

        @pl.when(z < nz - 1)
        def _():
            up(blk, q).start()

        @pl.when(z > 0)
        def _():
            down(blk, q).start()

    table_w[...] = table_ref[...].astype(F32)
    pieces = [table_w[pl.ds(core * half + k, width, stride=width), :] for k in range(half)]
    table_t = jnp.concatenate(pieces, axis=0).T.astype(BF16)
    jrow = jrow_ref[...].astype(F32)
    count = jnp.sum(srow, axis=1, keepdims=True)
    for i in range(res):
        norm = jrow * rmask_ref[blk * res + i].astype(F32) * count
        inv[i:i + 1, :] = 1.0 / jnp.maximum(norm, 1.0)

    def from_below(block, q):
        copy(block, q, 0, blk).wait_recv()
        cross(block, q).start()

        @pl.when(z < nz - 1)
        def _():
            up(block, q).start()

    def from_above(block, q):
        copy(block, q, 1, blk).wait_recv()
        cross(block, q).start()

        @pl.when(z > 0)
        def _():
            down(block, q).start()

    for hop in range(1, nz):
        for q in range(CHUNKS):
            each_hop(q, hop, from_below, from_above)

    pairs = res // 2
    for q in range(CHUNKS):
        for k in range(nz):
            copy(2 * k + 1 - side, q, 2, blk).wait_recv()
        base = q * part
        right_q = jnp.concatenate(
            [right_t[:, base + k].reshape(cols, rows) for k in range(part)], axis=0
        )
        table_q = table_t[:, base * width:(base + part) * width]
        for p in range(pairs):
            left_p = left_t[p * 2 * width:(p + 1) * 2 * width, :]
            outer = lax.dot_general(left_p, right_q, nt, preferred_element_type=F32).astype(BF16)
            both = [
                jnp.concatenate(
                    [
                        outer[u * width:(u + 1) * width, k * cols:(k + 1) * cols]
                        for k in range(part)
                    ],
                    axis=0,
                )
                for u in range(2)
            ]
            term = jnp.dot(table_q, jnp.concatenate(both, axis=1), preferred_element_type=F32)
            for u in range(2):
                at = pl.ds(p * 2 + u, table_t.shape[0], stride=res)
                piece = term[:, u * cols:(u + 1) * cols]
                if q == 0:
                    acc[at, :] = piece
                else:
                    acc[at, :] += piece

    count_rows = acc.shape[0] // 2
    other = pl.multiple_of((1 - core) * count_rows, count_rows)
    own = pl.multiple_of(core * count_rows, count_rows)
    away[...] = acc[pl.ds(other, count_rows), :].astype(away.dtype)
    swap = pltpu.make_async_remote_copy(
        src_ref=away, dst_ref=near, send_sem=swap_sem.at[0], recv_sem=swap_sem.at[1],
        device_id={"ch": 1 - core}, device_id_type=MESH,
    )
    swap.start()

    def sent_below(block, q):
        cross(block, q).wait_send()

        @pl.when(z < nz - 1)
        def _():
            up(block, q).wait_send()

    def sent_above(block, q):
        cross(block, q).wait_send()

        @pl.when(z > 0)
        def _():
            down(block, q).wait_send()

    for q in range(CHUNKS):
        cross(blk, q).wait_send()

        @pl.when(z < nz - 1)
        def _():
            up(blk, q).wait_send()

        @pl.when(z > 0)
        def _():
            down(blk, q).wait_send()

        for hop in range(1, nz):
            each_hop(q, hop, sent_below, sent_above)

    swap.wait()
    total = acc[pl.ds(own, count_rows), :] + near[...].astype(F32)
    total = total.reshape(count_rows // res, res, cols) * inv[...][None]
    out_ref[...] = total.astype(BF16)


def fused_shards(
    alignment_activity, sequence_mask, residue_mask, lower_weights, upper_weights, output_projector
):
    rows, res, feat = alignment_activity.shape
    width = lower_weights.shape[1]
    pair = output_projector.shape[1]
    nblk = lax.axis_size("blk")
    cols = nblk * res
    half = width // 2
    vmem = pl.BlockSpec(memory_space=pltpu.VMEM)
    return pl.pallas_call(
        functools.partial(fused, (nblk, rows, res, feat, width)),
        out_shape=jax.ShapeDtypeStruct((pair // 2, res, cols), BF16),
        in_specs=[vmem, vmem, vmem, pl.BlockSpec(memory_space=pltpu.SMEM), vmem, vmem, vmem],
        out_specs=vmem,
        scratch_shapes=[
            pltpu.VMEM((rows * res, 128), F32),
            pltpu.VMEM((res * width, rows), BF16),
            pltpu.VMEM((rows // 128, width * res, 128), F32),
            pltpu.VMEM((nblk, half, res, rows), BF16),
            pltpu.VMEM((width * width, pair), F32),
            pltpu.VMEM((pair * res, cols), F32),
            pltpu.VMEM((pair // 2 * res, cols), SWAP_TYPE),
            pltpu.VMEM((pair // 2 * res, cols), SWAP_TYPE),
            pltpu.VMEM((res, cols), F32),
            pltpu.SemaphoreType.DMA((nblk, CHUNKS)),
            pltpu.SemaphoreType.DMA((3, nblk, CHUNKS)),
            pltpu.SemaphoreType.DMA((2,)),
        ],
        compiler_params=pltpu.CompilerParams(
            collective_id=0, has_side_effects=True, vmem_limit_bytes=40 * 1024 * 1024
        ),
        name="outer_product_mean",
    )(
        alignment_activity,
        sequence_mask.reshape(1, rows),
        residue_mask.reshape(1, cols),
        residue_mask,
        lower_weights,
        upper_weights,
        output_projector,
    )


SWAP_TYPE = F32


def choose(*arrays):
    rows, res, _ = arrays[0].shape
    width = arrays[3].shape[1]
    nblk = lax.axis_size("blk")
    one_share = lax.axis_size("seq") == 1 and lax.axis_size("ch") == 2
    tiled = nblk % 2 == 0 and nblk * res == 128 and res % 16 == 0 and rows % 128 == 0
    if one_share and tiled and width % 32 == 0:
        return fused_shards(*arrays)
    return shards(*arrays)


def solution(mesh):
    in_specs = (P(("grp", "seq"), "blk", None), P("grp"), P("grp"), P(), P(), P())
    out_specs = P("ch", ("grp", "blk"), "seq")
    return jax.shard_map(choose, mesh=mesh, in_specs=in_specs, out_specs=out_specs, check_vma=False)
```

```python
import functools
import math

import jax
import jax.numpy as jnp
from jax import lax
from jax.experimental import pallas as pl
from jax.experimental.pallas import tpu as pltpu
from jax.sharding import PartitionSpec as P


def shards(
    alignment_activity, sequence_mask, residue_mask, lower_weights, upper_weights, output_projector
):
    local_rows, block_rows, channel_count = alignment_activity.shape
    proj_width = lower_weights.shape[1]
    pair_width = output_projector.shape[1]
    seq_count = lax.axis_size("seq")
    core_count = lax.axis_size("ch")
    seq_place = lax.axis_index("seq")
    blk_place = lax.axis_index("blk")
    core_place = lax.axis_index("ch")
    value_entries = alignment_activity.astype(jnp.float32)
    centred = value_entries - jnp.mean(value_entries, axis=-1, keepdims=True)
    variance = jnp.mean(centred * centred, axis=-1, keepdims=True)
    normed = (centred * lax.rsqrt(variance + 1e-05)).astype(jnp.bfloat16)
    rows_valid = lax.dynamic_slice_in_dim(sequence_mask, seq_place * local_rows, local_rows).astype(
        jnp.float32
    )
    res_valid = lax.dynamic_slice_in_dim(residue_mask, blk_place * block_rows, block_rows).astype(
        jnp.float32
    )
    weight = (rows_valid[:, None] * res_valid[None, :])[:, :, None]
    left_matrix = (
        jnp.einsum("sic,cd->sid", normed, lower_weights, preferred_element_type=jnp.float32)
        * weight
    ).astype(jnp.bfloat16)
    right = (
        jnp.einsum("sic,cd->sid", normed, upper_weights, preferred_element_type=jnp.float32)
        * weight
    ).astype(jnp.bfloat16)
    right_flat = right.reshape(local_rows, block_rows * proj_width)
    table = output_projector.reshape(proj_width, proj_width, pair_width)
    out_width = pair_width // core_count
    table_used = lax.dynamic_slice_in_dim(table, core_place * out_width, out_width, 2)
    used_channels = table_used.shape[2]
    piece = lax.all_gather(right_flat, "blk", axis=1, tiled=True)
    col_count = piece.shape[1] // proj_width
    block_cols = math.gcd(col_count, 128)
    block_count = col_count // block_cols
    stacked = piece.reshape(local_rows, block_count, block_cols, proj_width).transpose(1, 0, 2, 3)

    def one_block(right_part):
        outer = jnp.einsum(
            "sic,sjd->ijcd", left_matrix, right_part, preferred_element_type=jnp.float32
        ).astype(jnp.bfloat16)
        return jnp.einsum("ijcd,cde->eij", outer, table_used, preferred_element_type=jnp.float32)

    results = lax.map(one_block, stacked)
    partial_sum = results.transpose(1, 2, 0, 3).reshape(used_channels, block_rows, col_count)
    all_cols = partial_sum.shape[2]
    quarter_cols = all_cols // seq_count
    summed = lax.psum_scatter(
        partial_sum.astype(jnp.bfloat16), "seq", scatter_dimension=2, tiled=True
    ).astype(jnp.float32)
    count = jnp.sum(sequence_mask.astype(jnp.float32))
    col_valid = lax.dynamic_slice_in_dim(
        residue_mask, seq_place * quarter_cols, quarter_cols
    ).astype(jnp.float32)
    norm = res_valid[:, None] * col_valid[None, :] * count
    return (summed / jnp.maximum(norm, 1.0)[None]).astype(jnp.bfloat16)


F32 = jnp.float32
BF16 = jnp.bfloat16
CHUNKS = 2
VMEM_BYTES = 63 * 1024 * 1024
MESH = pl.DeviceIdType.MESH


def fused(
    sizes,
    x_hbm, srow_hbm, jrow_hbm, rmask_hbm, lower_hbm, upper_hbm, table_hbm,
    out_ref,
    x_ref, srow_ref, jrow_ref, rmask_ref, lower_ref, upper_ref, table_ref, normed_ref, left_t, right_w, right_t, table_w, outer_ref,
    acc, away, near, inv,
    load_sem, recv_sem, send_sem, swap_sem,
):
    nblk, rows, res, feat, width = sizes
    half = width // 2
    part = half // CHUNKS
    nz = nblk // 2
    cols = nblk * res
    lane_tiles = rows // 128
    groups = 4
    group = res // groups
    blk = lax.axis_index("blk")
    core = lax.axis_index("ch")
    z = blk // 2
    side = blk % 2
    across = z * 2 + 1 - side

    barrier = pltpu.get_barrier_semaphore()
    pl.semaphore_signal(barrier, inc=1, device_id={"blk": across}, device_id_type=MESH)
    pl.semaphore_signal(barrier, inc=1, device_id={"ch": 1 - core}, device_id_type=MESH)

    @pl.when(z > 0)
    def _():
        pl.semaphore_signal(barrier, inc=1, device_id={"blk": blk - 2}, device_id_type=MESH)

    @pl.when(z < nz - 1)
    def _():
        pl.semaphore_signal(barrier, inc=1, device_id={"blk": blk + 2}, device_id_type=MESH)

    loads = [
        pltpu.make_async_copy(x_hbm.at[pl.ds(g * group, group)], x_ref.at[pl.ds(g * group, group)], load_sem.at[g])
        for g in range(groups)
    ]
    early = ((upper_hbm, upper_ref), (srow_hbm, srow_ref), (rmask_hbm, rmask_ref))
    later = ((lower_hbm, lower_ref), (jrow_hbm, jrow_ref), (table_hbm, table_ref))
    smalls = [
        pltpu.make_async_copy(src, dst, load_sem.at[groups + k])
        for k, (src, dst) in enumerate(early + later)
    ]
    for load in smalls[:3] + loads + smalls[3:]:
        load.start()
    for load in smalls[:3]:
        load.wait()

    srow = srow_ref[...].astype(F32)
    upper_t = upper_ref[...]
    for i in range(res):
        if i % group == 0:
            loads[i // group].wait()
        x_i = x_ref[i].astype(F32)
        cent = x_i - jnp.mean(x_i, axis=0, keepdims=True)
        var = jnp.mean(cent * cent, axis=0, keepdims=True)
        normed = (cent * lax.rsqrt(var + 1e-05)).astype(BF16)
        normed_ref[i] = normed
        proj = jnp.dot(upper_t, normed, preferred_element_type=F32)
        proj = proj * (srow * rmask_ref[blk * res + i].astype(F32))
        for g in range(lane_tiles):
            right_w[g, pl.ds(i, width, stride=res), :] = proj[:, g * 128:(g + 1) * 128]
    mine = pl.ds(pl.multiple_of(core * (half * res), half * res), half * res)
    for g in range(lane_tiles):
        block = right_w[g, mine, :].astype(BF16).reshape(half, res, 128)
        right_t[blk, :, :, g * 128:(g + 1) * 128] = block

    peers = 2 + (z + nz - 1) // nz + (2 * nz - 2 - z) // nz
    pl.semaphore_wait(barrier, peers)

    def copy(block, q, way, target):
        ref = right_t.at[block, pl.ds(q * part, part)]
        return pltpu.make_async_remote_copy(
            src_ref=ref, dst_ref=ref,
            send_sem=send_sem.at[way, block, q], recv_sem=recv_sem.at[block, q],
            device_id={"blk": target}, device_id_type=MESH,
        )

    def up(block, q):
        return copy(block, q, 0, blk + 2)

    def down(block, q):
        return copy(block, q, 1, blk - 2)

    def cross(block, q):
        return copy(block, q, 2, across)

    def each_hop(q, hop, act_below, act_above):
        @pl.when(z >= hop)
        def _():
            act_below(blk - 2 * hop, q)

        @pl.when(z + hop < nz)
        def _():
            act_above(blk + 2 * hop, q)

    for q in range(CHUNKS):
        cross(blk, q).start()

        @pl.when(z < nz - 1)
        def _():
            up(blk, q).start()

        @pl.when(z > 0)
        def _():
            down(blk, q).start()

    for load in smalls[3:]:
        load.wait()
    lower_t = lower_ref[...]
    for i in range(res):
        proj = jnp.dot(lower_t, normed_ref[i], preferred_element_type=F32)
        proj = proj * (srow * rmask_ref[blk * res + i].astype(F32))
        left_t[i * width:(i + 1) * width, :] = proj.astype(BF16)

    table_w[...] = table_ref[...].astype(F32)
    pieces = [table_w[pl.ds(core * half + k, width, stride=width), :] for k in range(half)]
    table_t = jnp.concatenate(pieces, axis=0).T.astype(BF16)
    jrow = jrow_ref[...].astype(F32)
    count = jnp.sum(srow, axis=1, keepdims=True)
    for i in range(res):
        norm = jrow * rmask_ref[blk * res + i].astype(F32) * count
        inv[i:i + 1, :] = 1.0 / jnp.maximum(norm, 1.0)

    def from_below(block, q):
        copy(block, q, 0, blk).wait_recv()
        cross(block, q).start()

        @pl.when(z < nz - 1)
        def _():
            up(block, q).start()

    def from_above(block, q):
        copy(block, q, 1, blk).wait_recv()
        cross(block, q).start()

        @pl.when(z > 0)
        def _():
            down(block, q).start()

    for hop in range(1, nz):
        for q in range(CHUNKS):
            each_hop(q, hop, from_below, from_above)

    nt = (((1,), (1,)), ((), ()))
    pairs = res // 2
    for q in range(CHUNKS):
        for k in range(nz):
            copy(2 * k + 1 - side, q, 2, blk).wait_recv()
        base = q * part
        for k in range(base, base + part, 2):
            right_k = jnp.concatenate(
                [right_t[:, k + u].reshape(cols, rows) for u in range(2)], axis=0
            )
            outer = lax.dot_general(left_t[...], right_k, nt, preferred_element_type=F32)
            outer = outer.astype(BF16)
            for u in range(2):
                piece = outer[:, u * cols:(u + 1) * cols].reshape(res, width, cols)
                outer_ref[:, (k + u) * width:(k + u + 1) * width, :] = piece
        table_q = table_t[:, base * width:(base + part) * width]
        for p in range(pairs):
            both = [
                outer_ref[p * 2 + u, base * width:(base + part) * width, :] for u in range(2)
            ]
            term = jnp.dot(table_q, jnp.concatenate(both, axis=1), preferred_element_type=F32)
            for u in range(2):
                at = pl.ds(p * 2 + u, table_t.shape[0], stride=res)
                piece = term[:, u * cols:(u + 1) * cols]
                if q == 0:
                    acc[at, :] = piece
                else:
                    acc[at, :] += piece

    count_rows = acc.shape[0] // 2
    other = pl.multiple_of((1 - core) * count_rows, count_rows)
    own = pl.multiple_of(core * count_rows, count_rows)
    away[...] = acc[pl.ds(other, count_rows), :].astype(away.dtype)
    swap = pltpu.make_async_remote_copy(
        src_ref=away, dst_ref=near, send_sem=swap_sem.at[0], recv_sem=swap_sem.at[1],
        device_id={"ch": 1 - core}, device_id_type=MESH,
    )
    swap.start()

    def sent_below(block, q):
        cross(block, q).wait_send()

        @pl.when(z < nz - 1)
        def _():
            up(block, q).wait_send()

    def sent_above(block, q):
        cross(block, q).wait_send()

        @pl.when(z > 0)
        def _():
            down(block, q).wait_send()

    for q in range(CHUNKS):
        cross(blk, q).wait_send()

        @pl.when(z < nz - 1)
        def _():
            up(blk, q).wait_send()

        @pl.when(z > 0)
        def _():
            down(blk, q).wait_send()

        for hop in range(1, nz):
            each_hop(q, hop, sent_below, sent_above)

    swap.wait()
    total = acc[pl.ds(own, count_rows), :] + near[...].astype(F32)
    total = total.reshape(count_rows // res, res, cols) * inv[...][None]
    out_ref[...] = total.astype(BF16)


def fused_shards(
    alignment_activity, sequence_mask, residue_mask, lower_weights, upper_weights, output_projector
):
    rows, res, feat = alignment_activity.shape
    width = lower_weights.shape[1]
    pair = output_projector.shape[1]
    nblk = lax.axis_size("blk")
    cols = nblk * res
    half = width // 2
    vmem = pl.BlockSpec(memory_space=pltpu.VMEM)
    hbm = pl.BlockSpec(memory_space=pltpu.HBM)
    return pl.pallas_call(
        functools.partial(fused, (nblk, rows, res, feat, width)),
        out_shape=jax.ShapeDtypeStruct((pair // 2, res, cols), BF16),
        in_specs=[hbm] * 7,
        out_specs=vmem,
        scratch_shapes=[
            pltpu.VMEM((res, feat, rows), BF16),
            pltpu.VMEM((1, rows), jnp.int32),
            pltpu.VMEM((1, cols), jnp.int32),
            pltpu.SMEM((cols,), jnp.int32),
            pltpu.VMEM((width, feat), BF16),
            pltpu.VMEM((width, feat), BF16),
            pltpu.VMEM((width * width, pair), BF16),
            pltpu.VMEM((res, feat, rows), BF16),
            pltpu.VMEM((res * width, rows), BF16),
            pltpu.VMEM((rows // 128, width * res, 128), F32),
            pltpu.VMEM((nblk, half, res, rows), BF16),
            pltpu.VMEM((width * width, pair), F32),
            pltpu.VMEM((res, half * width, cols), BF16),
            pltpu.VMEM((pair * res, cols), F32),
            pltpu.VMEM((pair // 2 * res, cols), SWAP_TYPE),
            pltpu.VMEM((pair // 2 * res, cols), SWAP_TYPE),
            pltpu.VMEM((res, cols), F32),
            pltpu.SemaphoreType.DMA((10,)),
            pltpu.SemaphoreType.DMA((nblk, CHUNKS)),
            pltpu.SemaphoreType.DMA((3, nblk, CHUNKS)),
            pltpu.SemaphoreType.DMA((2,)),
        ],
        compiler_params=pltpu.CompilerParams(
            collective_id=0, has_side_effects=True, vmem_limit_bytes=VMEM_BYTES
        ),
        name="outer_product_mean",
    )(
        alignment_activity.transpose(1, 2, 0),
        sequence_mask.reshape(1, rows),
        residue_mask.reshape(1, cols),
        residue_mask,
        lower_weights.T,
        upper_weights.T,
        output_projector,
    )


SWAP_TYPE = F32


def choose(*arrays):
    rows, res, _ = arrays[0].shape
    width = arrays[3].shape[1]
    nblk = lax.axis_size("blk")
    one_share = lax.axis_size("seq") == 1 and lax.axis_size("ch") == 2
    tiled = nblk % 2 == 0 and nblk * res == 128 and res % 16 == 0 and rows % 128 == 0
    if one_share and tiled and width % 32 == 0:
        return fused_shards(*arrays)
    return shards(*arrays)


def solution(mesh):
    in_specs = (P(("grp", "seq"), "blk", None), P("grp"), P("grp"), P(), P(), P())
    out_specs = P("ch", ("grp", "blk"), "seq")
    return jax.shard_map(choose, mesh=mesh, in_specs=in_specs, out_specs=out_specs, check_vma=False)
```

```python
import functools
import math

import jax
import jax.numpy as jnp
from jax import lax
from jax.experimental import pallas as pl
from jax.experimental.pallas import tpu as pltpu
from jax.sharding import PartitionSpec as P


def shards(
    alignment_activity, sequence_mask, residue_mask, lower_weights, upper_weights, output_projector
):
    local_rows, block_rows, channel_count = alignment_activity.shape
    proj_width = lower_weights.shape[1]
    pair_width = output_projector.shape[1]
    seq_count = lax.axis_size("seq")
    core_count = lax.axis_size("ch")
    seq_place = lax.axis_index("seq")
    blk_place = lax.axis_index("blk")
    core_place = lax.axis_index("ch")
    value_entries = alignment_activity.astype(jnp.float32)
    centred = value_entries - jnp.mean(value_entries, axis=-1, keepdims=True)
    variance = jnp.mean(centred * centred, axis=-1, keepdims=True)
    normed = (centred * lax.rsqrt(variance + 1e-05)).astype(jnp.bfloat16)
    rows_valid = lax.dynamic_slice_in_dim(sequence_mask, seq_place * local_rows, local_rows).astype(
        jnp.float32
    )
    res_valid = lax.dynamic_slice_in_dim(residue_mask, blk_place * block_rows, block_rows).astype(
        jnp.float32
    )
    weight = (rows_valid[:, None] * res_valid[None, :])[:, :, None]
    left_matrix = (
        jnp.einsum("sic,cd->sid", normed, lower_weights, preferred_element_type=jnp.float32)
        * weight
    ).astype(jnp.bfloat16)
    right = (
        jnp.einsum("sic,cd->sid", normed, upper_weights, preferred_element_type=jnp.float32)
        * weight
    ).astype(jnp.bfloat16)
    right_flat = right.reshape(local_rows, block_rows * proj_width)
    table = output_projector.reshape(proj_width, proj_width, pair_width)
    out_width = pair_width // core_count
    table_used = lax.dynamic_slice_in_dim(table, core_place * out_width, out_width, 2)
    used_channels = table_used.shape[2]
    piece = lax.all_gather(right_flat, "blk", axis=1, tiled=True)
    col_count = piece.shape[1] // proj_width
    block_cols = math.gcd(col_count, 128)
    block_count = col_count // block_cols
    stacked = piece.reshape(local_rows, block_count, block_cols, proj_width).transpose(1, 0, 2, 3)

    def one_block(right_part):
        outer = jnp.einsum(
            "sic,sjd->ijcd", left_matrix, right_part, preferred_element_type=jnp.float32
        ).astype(jnp.bfloat16)
        return jnp.einsum("ijcd,cde->eij", outer, table_used, preferred_element_type=jnp.float32)

    results = lax.map(one_block, stacked)
    partial_sum = results.transpose(1, 2, 0, 3).reshape(used_channels, block_rows, col_count)
    all_cols = partial_sum.shape[2]
    quarter_cols = all_cols // seq_count
    summed = lax.psum_scatter(
        partial_sum.astype(jnp.bfloat16), "seq", scatter_dimension=2, tiled=True
    ).astype(jnp.float32)
    count = jnp.sum(sequence_mask.astype(jnp.float32))
    col_valid = lax.dynamic_slice_in_dim(
        residue_mask, seq_place * quarter_cols, quarter_cols
    ).astype(jnp.float32)
    norm = res_valid[:, None] * col_valid[None, :] * count
    return (summed / jnp.maximum(norm, 1.0)[None]).astype(jnp.bfloat16)


F32 = jnp.float32
BF16 = jnp.bfloat16
CHUNKS = 2
VMEM_BYTES = 63 * 1024 * 1024
MESH = pl.DeviceIdType.MESH


def fused(
    sizes,
    x_hbm, srow_hbm, jrow_hbm, rmask_hbm, lower_hbm, upper_hbm, table_hbm,
    out_ref,
    x_ref, srow_ref, jrow_ref, rmask_ref, lower_ref, upper_ref, table_ref, normed_ref, left_t, right_w, right_t, table_w, outer_ref,
    acc, near, inv,
    load_sem, recv_sem, send_sem, swap_sem,
):
    nblk, rows, res, feat, width = sizes
    half = width // 2
    part = half // CHUNKS
    nz = nblk // 2
    cols = nblk * res
    lane_tiles = rows // 128
    groups = 4
    group = res // groups
    blk = lax.axis_index("blk")
    core = lax.axis_index("ch")
    z = blk // 2
    side = blk % 2
    across = z * 2 + 1 - side

    barrier = pltpu.get_barrier_semaphore()
    pl.semaphore_signal(barrier, inc=1, device_id={"blk": across}, device_id_type=MESH)
    pl.semaphore_signal(barrier, inc=1, device_id={"ch": 1 - core}, device_id_type=MESH)

    @pl.when(z > 0)
    def _():
        pl.semaphore_signal(barrier, inc=1, device_id={"blk": blk - 2}, device_id_type=MESH)

    @pl.when(z < nz - 1)
    def _():
        pl.semaphore_signal(barrier, inc=1, device_id={"blk": blk + 2}, device_id_type=MESH)

    loads = [
        pltpu.make_async_copy(x_hbm.at[pl.ds(g * group, group)], x_ref.at[pl.ds(g * group, group)], load_sem.at[g])
        for g in range(groups)
    ]
    early = ((upper_hbm, upper_ref), (srow_hbm, srow_ref), (rmask_hbm, rmask_ref))
    later = ((lower_hbm, lower_ref), (jrow_hbm, jrow_ref), (table_hbm, table_ref))
    smalls = [
        pltpu.make_async_copy(src, dst, load_sem.at[groups + k])
        for k, (src, dst) in enumerate(early + later)
    ]
    for load in smalls[:3] + loads + smalls[3:]:
        load.start()
    for load in smalls[:3]:
        load.wait()

    srow = srow_ref[...].astype(F32)
    upper_t = upper_ref[...]
    for i in range(res):
        if i % group == 0:
            loads[i // group].wait()
        x_i = x_ref[i].astype(F32)
        cent = x_i - jnp.mean(x_i, axis=0, keepdims=True)
        var = jnp.mean(cent * cent, axis=0, keepdims=True)
        normed = (cent * lax.rsqrt(var + 1e-05)).astype(BF16)
        normed_ref[i] = normed
        proj = jnp.dot(upper_t, normed, preferred_element_type=F32)
        proj = proj * (srow * rmask_ref[blk * res + i].astype(F32))
        for g in range(lane_tiles):
            right_w[g, pl.ds(i, width, stride=res), :] = proj[:, g * 128:(g + 1) * 128]
    mine = pl.ds(pl.multiple_of(core * (half * res), half * res), half * res)
    for g in range(lane_tiles):
        block = right_w[g, mine, :].astype(BF16).reshape(half, res, 128)
        right_t[blk, :, :, g * 128:(g + 1) * 128] = block

    peers = 2 + (z + nz - 1) // nz + (2 * nz - 2 - z) // nz
    pl.semaphore_wait(barrier, peers)

    def copy(block, q, way, target):
        ref = right_t.at[block, pl.ds(q * part, part)]
        return pltpu.make_async_remote_copy(
            src_ref=ref, dst_ref=ref,
            send_sem=send_sem.at[way, block, q], recv_sem=recv_sem.at[block, q],
            device_id={"blk": target}, device_id_type=MESH,
        )

    def up(block, q):
        return copy(block, q, 0, blk + 2)

    def down(block, q):
        return copy(block, q, 1, blk - 2)

    def cross(block, q):
        return copy(block, q, 2, across)

    def each_hop(q, hop, act_below, act_above):
        @pl.when(z >= hop)
        def _():
            act_below(blk - 2 * hop, q, hop)

        @pl.when(z + hop < nz)
        def _():
            act_above(blk + 2 * hop, q, hop)

    for q in range(CHUNKS):
        cross(blk, q).start()

        @pl.when(z < nz - 1)
        def _():
            up(blk, q).start()

        @pl.when(z > 0)
        def _():
            down(blk, q).start()

    for load in smalls[3:]:
        load.wait()
    lower_t = lower_ref[...]
    for i in range(res):
        proj = jnp.dot(lower_t, normed_ref[i], preferred_element_type=F32)
        proj = proj * (srow * rmask_ref[blk * res + i].astype(F32))
        left_t[i * width:(i + 1) * width, :] = proj.astype(BF16)

    table_w[...] = table_ref[...].astype(F32)
    pieces = [table_w[pl.ds(core * half + k, width, stride=width), :] for k in range(half)]
    pair = table_w.shape[1]
    turned = pltpu.roll(jnp.concatenate(pieces, axis=0), core * (pair // 2), axis=1)
    table_t = turned.T.astype(BF16)
    jrow = jrow_ref[...].astype(F32)
    count = jnp.sum(srow, axis=1, keepdims=True)
    for i in range(res):
        norm = jrow * rmask_ref[blk * res + i].astype(F32) * count
        inv[i:i + 1, :] = 1.0 / jnp.maximum(norm, 1.0)

    even = z % 2 == 0
    last = CHUNKS - 1
    mate = blk + 2 - 4 * (z % 2)

    def relay(block):
        return copy(block, last, 3, mate)

    def cross_below(block, q, hop, act):
        if hop == 1 and q == last:
            pl.when(even)(lambda: act(cross(block, q)))
        else:
            act(cross(block, q))

    def cross_above(block, q, hop, act):
        if hop == 1 and q == last:
            pl.when(z % 2 == 1)(lambda: act(cross(block, q)))
        else:
            act(cross(block, q))

    def start(made):
        made.start()

    def sent(made):
        made.wait_send()

    def from_below(block, q, hop):
        copy(block, q, 0, blk).wait_recv()
        cross_below(block, q, hop, start)

        @pl.when(z < nz - 1)
        def _():
            up(block, q).start()

    def from_above(block, q, hop):
        copy(block, q, 1, blk).wait_recv()
        cross_above(block, q, hop, start)

        @pl.when(z > 0)
        def _():
            down(block, q).start()

    for hop in range(1, nz):
        for q in range(CHUNKS):
            each_hop(q, hop, from_below, from_above)
        if hop == 1:
            copy(across, last, 2, blk).wait_recv()
            relay(across).start()

    def swap(h):
        return pltpu.make_async_remote_copy(
            src_ref=acc.at[1, h], dst_ref=near.at[h],
            send_sem=swap_sem.at[0, h], recv_sem=swap_sem.at[1, h],
            device_id={"ch": 1 - core}, device_id_type=MESH,
        )

    nt = (((1,), (1,)), ((), ()))
    pairs = res // 2
    for q in range(CHUNKS):
        for k in range(nz):
            if q == last:
                @pl.when(z != k)
                def _():
                    copy(2 * k + 1 - side, q, 2, blk).wait_recv()
            else:
                copy(2 * k + 1 - side, q, 2, blk).wait_recv()
        base = q * part
        for k in range(base, base + part, 2):
            right_k = jnp.concatenate(
                [right_t[:, k + u].reshape(cols, rows) for u in range(2)], axis=0
            )
            outer = lax.dot_general(left_t[...], right_k, nt, preferred_element_type=F32)
            outer = outer.astype(BF16)
            for u in range(2):
                piece = outer[:, u * cols:(u + 1) * cols].reshape(res, width, cols)
                outer_ref[:, (k + u) * width:(k + u + 1) * width, :] = piece
        table_q = table_t[:, base * width:(base + part) * width]
        for p in range(pairs):
            both = [
                outer_ref[p * 2 + u, base * width:(base + part) * width, :] for u in range(2)
            ]
            term = jnp.dot(table_q, jnp.concatenate(both, axis=1), preferred_element_type=F32)
            for u in range(2):
                i = p * 2 + u
                at = pl.ds(i % 8, pair // 2, stride=8)
                for g in range(2):
                    piece = term[g * (pair // 2):(g + 1) * (pair // 2), u * cols:(u + 1) * cols]
                    if q > 0:
                        piece = piece + acc[g, i // 8, at, :]
                    acc[g, i // 8, at, :] = piece
            if q == last and p % 4 == 3:
                swap(p // 4).start()

    def sent_below(block, q, hop):
        cross_below(block, q, hop, sent)

        @pl.when(z < nz - 1)
        def _():
            up(block, q).wait_send()

    def sent_above(block, q, hop):
        cross_above(block, q, hop, sent)

        @pl.when(z > 0)
        def _():
            down(block, q).wait_send()

    for q in range(CHUNKS):
        cross(blk, q).wait_send()

        @pl.when(z < nz - 1)
        def _():
            up(blk, q).wait_send()

        @pl.when(z > 0)
        def _():
            down(blk, q).wait_send()

        for hop in range(1, nz):
            each_hop(q, hop, sent_below, sent_above)
    relay(across).wait_send()

    sums = []
    for h in range(res // 8):
        swap(h).wait()
        total = (acc[0, h] + near[h]).reshape(pair // 2, 8, cols)
        sums.append(total * inv[h * 8:(h + 1) * 8, :][None])
    out_ref[...] = jnp.concatenate(sums, axis=1).astype(BF16)


def fused_shards(
    alignment_activity, sequence_mask, residue_mask, lower_weights, upper_weights, output_projector
):
    rows, res, feat = alignment_activity.shape
    width = lower_weights.shape[1]
    pair = output_projector.shape[1]
    nblk = lax.axis_size("blk")
    cols = nblk * res
    half = width // 2
    vmem = pl.BlockSpec(memory_space=pltpu.VMEM)
    hbm = pl.BlockSpec(memory_space=pltpu.HBM)
    return pl.pallas_call(
        functools.partial(fused, (nblk, rows, res, feat, width)),
        out_shape=jax.ShapeDtypeStruct((pair // 2, res, cols), BF16),
        in_specs=[hbm] * 7,
        out_specs=vmem,
        scratch_shapes=[
            pltpu.VMEM((res, feat, rows), BF16),
            pltpu.VMEM((1, rows), jnp.int32),
            pltpu.VMEM((1, cols), jnp.int32),
            pltpu.SMEM((cols,), jnp.int32),
            pltpu.VMEM((width, feat), BF16),
            pltpu.VMEM((width, feat), BF16),
            pltpu.VMEM((width * width, pair), BF16),
            pltpu.VMEM((res, feat, rows), BF16),
            pltpu.VMEM((res * width, rows), BF16),
            pltpu.VMEM((rows // 128, width * res, 128), F32),
            pltpu.VMEM((nblk, half, res, rows), BF16),
            pltpu.VMEM((width * width, pair), F32),
            pltpu.VMEM((res, half * width, cols), BF16),
            pltpu.VMEM((2, res // 8, pair // 2 * 8, cols), F32),
            pltpu.VMEM((res // 8, pair // 2 * 8, cols), F32),
            pltpu.VMEM((res, cols), F32),
            pltpu.SemaphoreType.DMA((10,)),
            pltpu.SemaphoreType.DMA((nblk, CHUNKS)),
            pltpu.SemaphoreType.DMA((4, nblk, CHUNKS)),
            pltpu.SemaphoreType.DMA((2, res // 8)),
        ],
        compiler_params=pltpu.CompilerParams(
            collective_id=0, has_side_effects=True, vmem_limit_bytes=VMEM_BYTES
        ),
        name="outer_product_mean",
    )(
        alignment_activity.transpose(1, 2, 0),
        sequence_mask.reshape(1, rows),
        residue_mask.reshape(1, cols),
        residue_mask,
        lower_weights.T,
        upper_weights.T,
        output_projector,
    )


def choose(*arrays):
    rows, res, _ = arrays[0].shape
    width = arrays[3].shape[1]
    nblk = lax.axis_size("blk")
    one_share = lax.axis_size("seq") == 1 and lax.axis_size("ch") == 2
    tiled = nblk % 4 == 0 and nblk * res == 128 and res % 16 == 0 and rows % 128 == 0
    if one_share and tiled and width % 32 == 0:
        return fused_shards(*arrays)
    return shards(*arrays)


def solution(mesh):
    in_specs = (P(("grp", "seq"), "blk", None), P("grp"), P("grp"), P(), P(), P())
    out_specs = P("ch", ("grp", "blk"), "seq")
    return jax.shard_map(choose, mesh=mesh, in_specs=in_specs, out_specs=out_specs, check_vma=False)
```

```python
import functools
import math

import jax
import jax.numpy as jnp
from jax import lax
from jax.experimental import pallas as pl
from jax.experimental.pallas import tpu as pltpu
from jax.sharding import PartitionSpec as P


def shards(
    alignment_activity, sequence_mask, residue_mask, lower_weights, upper_weights, output_projector
):
    local_rows, block_rows, channel_count = alignment_activity.shape
    proj_width = lower_weights.shape[1]
    pair_width = output_projector.shape[1]
    seq_count = lax.axis_size("seq")
    core_count = lax.axis_size("ch")
    seq_place = lax.axis_index("seq")
    blk_place = lax.axis_index("blk")
    core_place = lax.axis_index("ch")
    value_entries = alignment_activity.astype(jnp.float32)
    centred = value_entries - jnp.mean(value_entries, axis=-1, keepdims=True)
    variance = jnp.mean(centred * centred, axis=-1, keepdims=True)
    normed = (centred * lax.rsqrt(variance + 1e-05)).astype(jnp.bfloat16)
    rows_valid = lax.dynamic_slice_in_dim(sequence_mask, seq_place * local_rows, local_rows).astype(
        jnp.float32
    )
    res_valid = lax.dynamic_slice_in_dim(residue_mask, blk_place * block_rows, block_rows).astype(
        jnp.float32
    )
    weight = (rows_valid[:, None] * res_valid[None, :])[:, :, None]
    left_matrix = (
        jnp.einsum("sic,cd->sid", normed, lower_weights, preferred_element_type=jnp.float32)
        * weight
    ).astype(jnp.bfloat16)
    right = (
        jnp.einsum("sic,cd->sid", normed, upper_weights, preferred_element_type=jnp.float32)
        * weight
    ).astype(jnp.bfloat16)
    right_flat = right.reshape(local_rows, block_rows * proj_width)
    table = output_projector.reshape(proj_width, proj_width, pair_width)
    out_width = pair_width // core_count
    table_used = lax.dynamic_slice_in_dim(table, core_place * out_width, out_width, 2)
    used_channels = table_used.shape[2]
    piece = lax.all_gather(right_flat, "blk", axis=1, tiled=True)
    col_count = piece.shape[1] // proj_width
    block_cols = math.gcd(col_count, 128)
    block_count = col_count // block_cols
    stacked = piece.reshape(local_rows, block_count, block_cols, proj_width).transpose(1, 0, 2, 3)

    def one_block(right_part):
        outer = jnp.einsum(
            "sic,sjd->ijcd", left_matrix, right_part, preferred_element_type=jnp.float32
        ).astype(jnp.bfloat16)
        return jnp.einsum("ijcd,cde->eij", outer, table_used, preferred_element_type=jnp.float32)

    results = lax.map(one_block, stacked)
    partial_sum = results.transpose(1, 2, 0, 3).reshape(used_channels, block_rows, col_count)
    all_cols = partial_sum.shape[2]
    quarter_cols = all_cols // seq_count
    summed = lax.psum_scatter(
        partial_sum.astype(jnp.bfloat16), "seq", scatter_dimension=2, tiled=True
    ).astype(jnp.float32)
    count = jnp.sum(sequence_mask.astype(jnp.float32))
    col_valid = lax.dynamic_slice_in_dim(
        residue_mask, seq_place * quarter_cols, quarter_cols
    ).astype(jnp.float32)
    norm = res_valid[:, None] * col_valid[None, :] * count
    return (summed / jnp.maximum(norm, 1.0)[None]).astype(jnp.bfloat16)


F32 = jnp.float32
BF16 = jnp.bfloat16
CHUNKS = 4
VMEM_BYTES = 40 * 1024 * 1024
MESH = pl.DeviceIdType.MESH


def fused(
    sizes,
    x_hbm, srow_hbm, jrow_hbm, rmask_hbm, lower_hbm, upper_hbm, table_hbm,
    out_ref,
    x_ref, srow_ref, jrow_ref, rmask_ref, lower_ref, upper_ref, table_ref, normed_ref, left_t, right_w, right_t, table_w, outer_ref,
    acc, near, inv,
    load_sem, recv_sem, send_sem, swap_sem,
):
    nblk, rows, res, feat, width = sizes
    half = width // 2
    part = half // CHUNKS
    nz = nblk // 2
    cols = nblk * res
    lane_tiles = rows // 128
    groups = 4
    group = res // groups
    blk = lax.axis_index("blk")
    core = lax.axis_index("ch")
    z = blk // 2
    side = blk % 2
    across = z * 2 + 1 - side

    barrier = pltpu.get_barrier_semaphore()
    pl.semaphore_signal(barrier, inc=1, device_id={"blk": across}, device_id_type=MESH)
    pl.semaphore_signal(barrier, inc=1, device_id={"ch": 1 - core}, device_id_type=MESH)

    @pl.when(z > 0)
    def _():
        pl.semaphore_signal(barrier, inc=1, device_id={"blk": blk - 2}, device_id_type=MESH)

    @pl.when(z < nz - 1)
    def _():
        pl.semaphore_signal(barrier, inc=1, device_id={"blk": blk + 2}, device_id_type=MESH)

    loads = [
        pltpu.make_async_copy(x_hbm.at[pl.ds(g * group, group)], x_ref.at[pl.ds(g * group, group)], load_sem.at[g])
        for g in range(groups)
    ]
    early = ((upper_hbm, upper_ref), (srow_hbm, srow_ref), (rmask_hbm, rmask_ref))
    later = ((lower_hbm, lower_ref), (jrow_hbm, jrow_ref), (table_hbm, table_ref))
    smalls = [
        pltpu.make_async_copy(src, dst, load_sem.at[groups + k])
        for k, (src, dst) in enumerate(early + later)
    ]
    for load in smalls[:3] + loads + smalls[3:]:
        load.start()
    for load in smalls[:3]:
        load.wait()

    srow = srow_ref[...].astype(F32)
    upper_t = upper_ref[...]
    for i in range(res):
        if i % group == 0:
            loads[i // group].wait()
        x_i = x_ref[i].astype(F32)
        cent = x_i - jnp.mean(x_i, axis=0, keepdims=True)
        var = jnp.mean(cent * cent, axis=0, keepdims=True)
        normed = (cent * lax.rsqrt(var + 1e-05)).astype(BF16)
        normed_ref[i] = normed
        proj = jnp.dot(upper_t, normed, preferred_element_type=F32)
        proj = proj * (srow * rmask_ref[blk * res + i].astype(F32))
        for g in range(lane_tiles):
            right_w[g, pl.ds(i, width, stride=res), :] = proj[:, g * 128:(g + 1) * 128]
    mine = pl.ds(pl.multiple_of(core * (half * res), half * res), half * res)
    for g in range(lane_tiles):
        block = right_w[g, mine, :].astype(BF16).reshape(half, res, 128)
        right_t[blk, :, :, g * 128:(g + 1) * 128] = block

    peers = 2 + (z + nz - 1) // nz + (2 * nz - 2 - z) // nz
    pl.semaphore_wait(barrier, peers)

    def copy(block, q, way, target):
        ref = right_t.at[block, pl.ds(q * part, part)]
        return pltpu.make_async_remote_copy(
            src_ref=ref, dst_ref=ref,
            send_sem=send_sem.at[way, block, q], recv_sem=recv_sem.at[block, q],
            device_id={"blk": target}, device_id_type=MESH,
        )

    def up(block, q):
        return copy(block, q, 0, blk + 2)

    def down(block, q):
        return copy(block, q, 1, blk - 2)

    def cross(block, q):
        return copy(block, q, 2, across)

    def each_hop(q, hop, act_below, act_above):
        @pl.when(z >= hop)
        def _():
            act_below(blk - 2 * hop, q)

        @pl.when(z + hop < nz)
        def _():
            act_above(blk + 2 * hop, q)

    for q in range(CHUNKS):
        cross(blk, q).start()

        @pl.when(z < nz - 1)
        def _():
            up(blk, q).start()

        @pl.when(z > 0)
        def _():
            down(blk, q).start()

    for load in smalls[3:]:
        load.wait()
    lower_t = lower_ref[...]
    for i in range(res):
        proj = jnp.dot(lower_t, normed_ref[i], preferred_element_type=F32)
        proj = proj * (srow * rmask_ref[blk * res + i].astype(F32))
        left_t[i * width:(i + 1) * width, :] = proj.astype(BF16)

    table_w[...] = table_ref[...].astype(F32)
    pieces = [table_w[pl.ds(core * half + k, width, stride=width), :] for k in range(half)]
    pair = table_w.shape[1]
    turned = pltpu.roll(jnp.concatenate(pieces, axis=0), core * (pair // 2), axis=1)
    table_t = turned.T.astype(BF16)
    jrow = jrow_ref[...].astype(F32)
    count = jnp.sum(srow, axis=1, keepdims=True)
    for i in range(res):
        norm = jrow * rmask_ref[blk * res + i].astype(F32) * count
        inv[i:i + 1, :] = 1.0 / jnp.maximum(norm, 1.0)

    last = CHUNKS - 1

    def from_below(block, q):
        copy(block, q, 0, blk).wait_recv()
        cross(block, q).start()

        @pl.when(z < nz - 1)
        def _():
            up(block, q).start()

    def from_above(block, q):
        copy(block, q, 1, blk).wait_recv()
        cross(block, q).start()

        @pl.when(z > 0)
        def _():
            down(block, q).start()

    for hop in range(1, nz):
        for q in range(CHUNKS):
            each_hop(q, hop, from_below, from_above)

    def swap(h):
        return pltpu.make_async_remote_copy(
            src_ref=acc.at[1, h], dst_ref=near.at[h],
            send_sem=swap_sem.at[0, h], recv_sem=swap_sem.at[1, h],
            device_id={"ch": 1 - core}, device_id_type=MESH,
        )

    nt = (((1,), (1,)), ((), ()))
    pairs = res // 2
    for q in range(CHUNKS):
        for k in range(nz):
            copy(2 * k + 1 - side, q, 2, blk).wait_recv()
        base = q * part
        for k in range(base, base + part, 2):
            right_k = jnp.concatenate(
                [right_t[:, k + u].reshape(cols, rows) for u in range(2)], axis=0
            )
            outer = lax.dot_general(left_t[...], right_k, nt, preferred_element_type=F32)
            outer = outer.astype(BF16)
            for u in range(2):
                piece = outer[:, u * cols:(u + 1) * cols].reshape(res, width, cols)
                outer_ref[:, (k + u) * width:(k + u + 1) * width, :] = piece
        if q < last - 1:
            continue
        first = 0 if q < last else base * width
        depth = (base + part) * width
        table_q = table_t[:, first:depth]
        for p in range(pairs):
            both = [
                outer_ref[p * 2 + u, first:depth, :] for u in range(2)
            ]
            term = jnp.dot(table_q, jnp.concatenate(both, axis=1), preferred_element_type=F32)
            for u in range(2):
                i = p * 2 + u
                at = pl.ds(i % 8, pair // 2, stride=8)
                for g in range(2):
                    piece = term[g * (pair // 2):(g + 1) * (pair // 2), u * cols:(u + 1) * cols]
                    if q == last:
                        piece = piece + acc[g, i // 8, at, :]
                    acc[g, i // 8, at, :] = piece
            if q == last and p % 4 == 3:
                swap(p // 4).start()

    def sent_below(block, q):
        cross(block, q).wait_send()

        @pl.when(z < nz - 1)
        def _():
            up(block, q).wait_send()

    def sent_above(block, q):
        cross(block, q).wait_send()

        @pl.when(z > 0)
        def _():
            down(block, q).wait_send()

    for q in range(CHUNKS):
        cross(blk, q).wait_send()

        @pl.when(z < nz - 1)
        def _():
            up(blk, q).wait_send()

        @pl.when(z > 0)
        def _():
            down(blk, q).wait_send()

        for hop in range(1, nz):
            each_hop(q, hop, sent_below, sent_above)

    sums = []
    for h in range(res // 8):
        swap(h).wait()
        total = (acc[0, h] + near[h]).reshape(pair // 2, 8, cols)
        sums.append(total * inv[h * 8:(h + 1) * 8, :][None])
    out_ref[...] = jnp.concatenate(sums, axis=1).astype(BF16)


def fused_shards(
    alignment_activity, sequence_mask, residue_mask, lower_weights, upper_weights, output_projector
):
    rows, res, feat = alignment_activity.shape
    width = lower_weights.shape[1]
    pair = output_projector.shape[1]
    nblk = lax.axis_size("blk")
    cols = nblk * res
    half = width // 2
    vmem = pl.BlockSpec(memory_space=pltpu.VMEM)
    hbm = pl.BlockSpec(memory_space=pltpu.HBM)
    return pl.pallas_call(
        functools.partial(fused, (nblk, rows, res, feat, width)),
        out_shape=jax.ShapeDtypeStruct((pair // 2, res, cols), BF16),
        in_specs=[hbm] * 7,
        out_specs=vmem,
        scratch_shapes=[
            pltpu.VMEM((res, feat, rows), BF16),
            pltpu.VMEM((1, rows), jnp.int32),
            pltpu.VMEM((1, cols), jnp.int32),
            pltpu.SMEM((cols,), jnp.int32),
            pltpu.VMEM((width, feat), BF16),
            pltpu.VMEM((width, feat), BF16),
            pltpu.VMEM((width * width, pair), BF16),
            pltpu.VMEM((res, feat, rows), BF16),
            pltpu.VMEM((res * width, rows), BF16),
            pltpu.VMEM((rows // 128, width * res, 128), F32),
            pltpu.VMEM((nblk, half, res, rows), BF16),
            pltpu.VMEM((width * width, pair), F32),
            pltpu.VMEM((res, half * width, cols), BF16),
            pltpu.VMEM((2, res // 8, pair // 2 * 8, cols), F32),
            pltpu.VMEM((res // 8, pair // 2 * 8, cols), F32),
            pltpu.VMEM((res, cols), F32),
            pltpu.SemaphoreType.DMA((10,)),
            pltpu.SemaphoreType.DMA((nblk, CHUNKS)),
            pltpu.SemaphoreType.DMA((3, nblk, CHUNKS)),
            pltpu.SemaphoreType.DMA((2, res // 8)),
        ],
        compiler_params=pltpu.CompilerParams(
            collective_id=0, has_side_effects=True, vmem_limit_bytes=VMEM_BYTES
        ),
        name="outer_product_mean",
    )(
        *[
            pltpu.with_memory_space_constraint(array, pltpu.HBM)
            for array in (
                alignment_activity.transpose(1, 2, 0),
                sequence_mask.reshape(1, rows),
                residue_mask.reshape(1, cols),
                residue_mask,
                lower_weights.T,
                upper_weights.T,
                output_projector,
            )
        ]
    )


def choose(*arrays):
    rows, res, _ = arrays[0].shape
    width = arrays[3].shape[1]
    nblk = lax.axis_size("blk")
    one_share = lax.axis_size("seq") == 1 and lax.axis_size("ch") == 2
    tiled = nblk % 4 == 0 and nblk * res == 128 and res % 16 == 0 and rows % 128 == 0
    if one_share and tiled and width % 32 == 0:
        return fused_shards(*arrays)
    return shards(*arrays)


def solution(mesh):
    in_specs = (P(("grp", "seq"), "blk", None), P("grp"), P("grp"), P(), P(), P())
    out_specs = P("ch", ("grp", "blk"), "seq")
    return jax.shard_map(choose, mesh=mesh, in_specs=in_specs, out_specs=out_specs, check_vma=False)
```
